32 devices in a mesh: samp: 1, vert: 32 (over z, y, x, core).
Axes of the slice: x: 2, y: 2, z: 4, core: 2. Of those that a mesh axis runs over, the one named last changes fastest.
Arguments:
- inputs: bfloat16 [2, 131072, 128], P('samp', 'vert'), may hold values from -6 to 6
- cotangent: bfloat16 [2, 131072, 128], P('samp', 'vert'), may hold values from -6 to 6
- basis: bfloat16 [131072, 1024], P('vert'), may hold values from -0.03125 to 0.03125
- mode_weights: bfloat16 [1024, 128, 128], P('vert'), may hold values from -0.5 to 0.5
- w_up: bfloat16 [128, 512], replicated, may hold values from -0.5 to 0.5
- b_up: float32 [512], replicated, may hold values from -4 to 4
- w_down: bfloat16 [512, 128], replicated, may hold values from -0.25 to 0.25
Outputs:
- grad_input: bfloat16 [2, 131072, 128], P('samp', 'vert')
- grad_modes: float32 [1024, 128, 128], P('vert')
- grad_w_up: float32 [128, 512], replicated
- grad_b_up: float32 [512], replicated
- grad_w_down: float32 [512, 128], replicated
The draws below stay inside these ranges and needn't reach their ends.
All inputs are finite; a program needn't handle non-finite values.
Results may differ from the reference program's by a relative error of at most 0.0055.
Values may be sent and summed in bfloat16 or wider, within the bound.
A program may use at most 128 MiB of HBM per device.

```python
import jax
import jax.numpy as jnp
from jax import lax

C = 128
H = 512
K = 1024
VERTICES = 131072
SAMPLES = 2


def shard_levels(stream_key, extent, pieces, smallest, top_value):
    level, own = 1.0, jax.random.fold_in(stream_key, 6)
    for axis_at, blocks in pieces:
        steps = jnp.exp(jax.random.uniform(jax.random.fold_in(own, axis_at), (blocks,), jnp.float32, smallest / len(pieces), top_value / len(pieces)))
        level = level * jnp.repeat(steps, extent[axis_at] // blocks).reshape([-1 if axis == axis_at else 1 for axis in range(len(extent))])
    return level


def normal_values(own_key, dims, scale, most, shards=(), held_as=jnp.bfloat16):
    loudness = shard_levels(own_key, dims, shards, -0.22, 0.18) if shards else 1.0
    entries = jax.random.normal(own_key, dims, jnp.float32) * scale * loudness
    return jnp.minimum(jnp.maximum(entries, -most), most).astype(held_as)


def setup_inputs(seed: int = 0) -> dict:
    seeds = jax.random.split(jax.random.key(seed), 8)
    return {
        "inputs": normal_values(seeds[0], (SAMPLES, VERTICES, C), 1.0, 6.0, ((1, 32),)),
        "cotangent": normal_values(seeds[1], (SAMPLES, VERTICES, C), 1.0, 6.0, ((1, 32),)),
        "basis": normal_values(seeds[2], (VERTICES, K), (VERTICES // 4) ** -0.5, 0.03125, ((0, 32),)),
        "mode_weights": normal_values(seeds[3], (K, C, C), C ** -0.5, 0.5, ((0, 32),)),
        "w_up": normal_values(seeds[4], (C, H), C ** -0.5, 0.5),
        "b_up": normal_values(seeds[5], (H,), 1.0, 4.0, (), jnp.float32),
        "w_down": normal_values(seeds[6], (H, C), H ** -0.5, 0.25),
    }


def gelu_value(pre_act):
    inner = 0.7978845608 * (pre_act + 0.044715 * pre_act * pre_act * pre_act)
    return 0.5 * pre_act * (1.0 + jnp.tanh(inner))


def gelu_slope(pre_act):
    inner = 0.7978845608 * (pre_act + 0.044715 * pre_act * pre_act * pre_act)
    tangent = jnp.tanh(inner)
    return 0.5 * (1.0 + tangent) + 0.5 * pre_act * (1.0 - tangent * tangent) * 0.7978845608 * (1.0 + 3.0 * 0.044715 * pre_act * pre_act)


def reference(inputs, cotangent, basis, mode_weights, w_up, b_up, w_down):
    mixing = mode_weights.astype(jnp.float32)
    grad_modes = jnp.zeros((K, C, C), jnp.float32)
    grad_w_up = jnp.zeros((C, H), jnp.float32)
    grad_b_up = jnp.zeros((H,), jnp.float32)
    grad_w_down = jnp.zeros((H, C), jnp.float32)
    results = []
    for sample in range(SAMPLES):
        coeffs = jnp.dot(basis.T, inputs[sample], preferred_element_type=jnp.float32)
        grad_out = jnp.dot(basis.T, cotangent[sample], preferred_element_type=jnp.float32)
        grad_coef = jnp.einsum("kd,kcd->kc", grad_out, mixing, precision=lax.Precision.HIGHEST).astype(jnp.bfloat16)
        grad_modes = grad_modes + jnp.einsum("kc,kd->kcd", coeffs, grad_out, precision=lax.Precision.HIGHEST)
        spectral = jnp.dot(basis, grad_coef, preferred_element_type=jnp.float32)
        pre_act = jnp.dot(inputs[sample], w_up, preferred_element_type=jnp.float32) + b_up
        hidden = gelu_value(pre_act).astype(jnp.bfloat16)
        grad_hidden = jnp.dot(cotangent[sample], w_down.T, preferred_element_type=jnp.float32)
        grad_pre = (grad_hidden * gelu_slope(pre_act)).astype(jnp.bfloat16)
        pointwise = jnp.dot(grad_pre, w_up.T, preferred_element_type=jnp.float32)
        results.append((spectral + pointwise).astype(jnp.bfloat16))
        grad_w_up = grad_w_up + jnp.dot(inputs[sample].T, grad_pre, preferred_element_type=jnp.float32)
        grad_b_up = grad_b_up + jnp.sum(grad_pre.astype(jnp.float32), axis=0)
        grad_w_down = grad_w_down + jnp.dot(hidden.T, cotangent[sample], preferred_element_type=jnp.float32)
    grad_input = jnp.stack(results, axis=0)
    return (grad_input, grad_modes, grad_w_up, grad_b_up, grad_w_down)
```

```python
import functools

import jax
import jax.numpy as jnp
from jax import lax
from jax.experimental import pallas as pl
from jax.experimental.pallas import tpu as pltpu
from jax.sharding import PartitionSpec as P

F32 = jnp.float32
BF16 = jnp.bfloat16
MESH = pl.DeviceIdType.MESH
ROOT = 0.7978845608
CUBE = 0.044715


def radices_of(size):
    radices = []
    if size % 4 == 0:
        radices.append(4)
        size //= 4
    while size > 1:
        step = 2 if size % 2 == 0 else size
        radices.append(step)
        size //= step
    return tuple(radices) or (1,)


def dot(left, right, contract):
    return lax.dot_general(left, right, (contract, ((), ())), preferred_element_type=F32)


def layer_kernel(
    plan,
    inputs_hbm, cotangent_hbm, basis_hbm, modes_hbm, w_up, b_up, w_down,
    grad_input_hbm, grad_modes_hbm, grad_up, grad_bias, grad_down,
    xs, cs, xt, basis, modes, acc, pointwise, result, outer,
    up_acc, down_acc, bias_acc, gathered, natural, left_rows, right_rows, mixed,
    weights_all, in_sems, out_sems, send_sems, recv_sems, *stages,
):
    size, radices = plan["size"], plan["radices"]
    samples, here, chan = xs.shape
    hidden_units = w_up.shape[1]
    total_modes = basis.shape[1]
    owned = total_modes // size
    depth = len(radices)
    coef_f32 = stages[0:depth]
    coef_send = stages[depth:2 * depth]
    coef_recv = stages[2 * depth:3 * depth]
    weight_f32 = stages[3 * depth:4 * depth]
    weight_recv = stages[4 * depth:5 * depth]
    bias_slots = stages[5 * depth:6 * depth]

    me = lax.axis_index("vert")
    strides = [1] * depth
    for at in range(depth - 2, -1, -1):
        strides[at] = strides[at + 1] * radices[at + 1]
    digits = [lax.rem(lax.div(me, strides[at]), radices[at]) for at in range(depth)]

    def peer(at, shift):
        digit = lax.rem(digits[at] + shift, radices[at])
        return digit, {"vert": me + (digit - digits[at]) * strides[at]}

    load_steps = plan["load_steps"]
    load_rows = here // load_steps

    def loads(step):
        rows = pl.ds(pl.multiple_of(step * load_rows, load_rows), load_rows)
        return (
            pltpu.make_async_copy(inputs_hbm.at[:, rows], xs.at[:, rows], in_sems.at[0, step]),
            pltpu.make_async_copy(cotangent_hbm.at[:, rows], cs.at[:, rows], in_sems.at[1, step]),
            pltpu.make_async_copy(basis_hbm.at[rows], basis.at[rows], in_sems.at[2, step]),
        )

    for step in range(load_steps):
        for copy in loads(step):
            copy.start()
    modes_copy = pltpu.make_async_copy(modes_hbm, modes, in_sems.at[3, 0])
    modes_copy.start()

    barrier = pltpu.get_barrier_semaphore()
    peers = 0
    for at in range(depth):
        for shift in range(1, radices[at]):
            pl.semaphore_signal(barrier, inc=1, device_id=peer(at, shift)[1], device_id_type=MESH)
            peers += 1

    acc[...] = jnp.zeros_like(acc)
    up_acc[...] = jnp.zeros_like(up_acc)
    down_acc[...] = jnp.zeros_like(down_acc)
    bias_acc[...] = jnp.zeros_like(bias_acc)

    def project(step, carry):
        for copy in loads(step):
            copy.wait()
        rows = pl.ds(pl.multiple_of(step * load_rows, load_rows), load_rows)
        for s in range(samples):
            xt[2 * s * chan:(2 * s + 1) * chan, rows] = xs[s, rows, :].T
            xt[(2 * s + 1) * chan:(2 * s + 2) * chan, rows] = cs[s, rows, :].T
        acc[...] += dot(xt[:, rows], basis[rows, :], ((1,), (0,)))
        return carry

    lax.fori_loop(0, load_steps, project, 0)

    first = radices[-1]
    for block in range(total_modes // 128):
        tile = acc[:, block * 128:(block + 1) * 128].T
        for part in range(128 // owned):
            owner = block * (128 // owned) + part
            rows = tile[part * owned:(part + 1) * owned]
            coef_f32[0][owner % first, owner // first] = rows
            coef_send[0][owner % first, owner // first] = rows.astype(BF16)

    pl.semaphore_wait(barrier, peers)

    sem_at = [0]

    def exchange(at, pairs):
        copies = []
        for shift in range(1, radices[at]):
            digit, target = peer(at, shift)
            for source_of, dest in pairs:
                copies.append(pltpu.make_async_remote_copy(
                    src_ref=source_of(digit),
                    dst_ref=dest,
                    send_sem=send_sems.at[sem_at[0]],
                    recv_sem=recv_sems.at[sem_at[0]],
                    device_id=target,
                    device_id_type=MESH,
                ))
                sem_at[0] += 1
        for copy in copies:
            copy.start()
        return copies

    def finish(copies):
        for copy in copies:
            copy.wait()

    def scatter_start(turn):
        at = depth - 1 - turn
        return exchange(at, [(lambda digit: coef_send[turn].at[digit], coef_recv[turn].at[digits[at]])])

    def scatter_sum(turn, copies):
        at = depth - 1 - turn
        finish(copies)
        blocks = coef_f32[turn].shape[1]
        sums = []
        for block in range(blocks):
            value = coef_f32[turn][digits[at], block]
            for shift in range(1, radices[at]):
                value = value + coef_recv[turn][peer(at, shift)[0], block].astype(F32)
            if turn + 1 < depth:
                radix = radices[at - 1]
                coef_f32[turn + 1][block % radix, block // radix] = value
                coef_send[turn + 1][block % radix, block // radix] = value.astype(BF16)
            else:
                sums.append(value)
        return sums

    def weights_start(turn):
        at = depth - 1 - turn
        pairs = [
            (lambda digit: weight_f32[turn].at[digit], weight_recv[turn].at[digits[at]]),
            (lambda digit: bias_slots[turn].at[digits[at]], bias_slots[turn].at[digits[at]]),
        ]
        return exchange(at, pairs)

    def weights_sum(turn, copies):
        at = depth - 1 - turn
        finish(copies)
        blocks = weight_f32[turn].shape[1]
        for block in range(blocks):
            value = weight_f32[turn][digits[at], block]
            for shift in range(1, radices[at]):
                value = value + weight_recv[turn][peer(at, shift)[0], block]
            if turn + 1 < depth:
                radix = radices[at - 1]
                weight_f32[turn + 1][block % radix, block // radix] = value
            else:
                weights_all[tuple(reversed(digits))] = value
        bias = bias_slots[turn][0]
        for slot in range(1, radices[at]):
            bias = bias + bias_slots[turn][slot]
        if turn + 1 < depth:
            bias_slots[turn + 1][digits[at - 1]] = bias
        else:
            grad_bias[...] = jnp.sum(bias, axis=0, keepdims=True)

    def gather_start(turn, ref):
        held = ref.at[tuple(reversed(digits[turn:]))]
        return exchange(turn, [(lambda digit: held, held)])

    chunk = plan["chunk"]
    chunks = here // chunk

    def point(step, carry):
        rows = pl.ds(pl.multiple_of(step * chunk, chunk), chunk)
        for s in range(samples):
            z = dot(xs[s, rows, :], w_up[...], ((1,), (0,))) + b_up[...]
            square = z * z
            t = jnp.tanh(z * (ROOT + (ROOT * CUBE) * square))
            half = 0.5 * z
            plus = 1.0 + t
            hidden = (half * plus).astype(BF16)
            slope = plus * (0.5 + half * (1.0 - t) * (ROOT + (3.0 * ROOT * CUBE) * square))
            grad_hidden = dot(cs[s, rows, :], w_down[...], ((1,), (1,)))
            grad_pre = (grad_hidden * slope).astype(BF16)
            pointwise[s, rows, :] = dot(grad_pre, w_up[...], ((1,), (1,)))
            up_acc[...] += dot(xt[2 * s * chan:(2 * s + 1) * chan, rows], grad_pre, ((1,), (0,)))
            down_acc[...] += dot(xt[(2 * s + 1) * chan:(2 * s + 2) * chan, rows], hidden, ((1,), (0,)))
            bias_acc[...] += jnp.sum(grad_pre.astype(F32).reshape(chunk // 8, 8, hidden_units), axis=0)
        return carry

    for turn in range(depth):
        copies = scatter_start(turn)
        lax.fori_loop(chunks * turn // depth, chunks * (turn + 1) // depth, point, 0)
        sums = scatter_sum(turn, copies)
    owned_sums = sums[0]

    columns = plan["columns"]
    rows_each = 2 * chan * columns // size
    wide = hidden_units // columns
    for owner in range(size):
        row = (owner // columns) * rows_each
        source = up_acc if row < chan else down_acc
        row = row % chan
        column = (owner % columns) * wide
        weight_f32[0][owner % first, owner // first] = source[row:row + rows_each, column:column + wide]
    bias_slots[0][digits[-1]] = bias_acc[...]

    weight_copies = weights_start(0)

    left_rows[...] = jnp.zeros_like(left_rows)
    right_rows[...] = jnp.zeros_like(right_rows)
    for s in range(samples):
        coef = owned_sums[:, 2 * s * chan:(2 * s + 1) * chan]
        grad = owned_sums[:, (2 * s + 1) * chan:(2 * s + 2) * chan]
        coef_high = coef.astype(BF16).astype(F32)
        grad_high = grad.astype(BF16).astype(F32)
        left_rows[:, s, :] = coef_high
        left_rows[:, samples + s, :] = coef_high
        left_rows[:, 2 * samples + s, :] = coef - coef_high
        right_rows[:, s, :] = grad_high
        right_rows[:, samples + s, :] = grad - grad_high
        right_rows[:, 2 * samples + s, :] = grad_high
    modes_copy.wait()
    for k in range(owned):
        mixed[k] = dot(right_rows[k].astype(BF16), modes[k], ((1,), (1,)))
    mine = tuple(reversed(digits))
    for s in range(samples):
        value = mixed[:, s, :] + mixed[:, samples + s, :]
        gathered[mine + (slice(None), slice(s * chan, (s + 1) * chan))] = value.astype(BF16)

    per_turn = -(-owned // depth)
    for turn in range(depth):
        coef_copies = gather_start(turn, gathered)
        for k in range(turn * per_turn, min(owned, (turn + 1) * per_turn)):
            outer[k] = dot(left_rows[k].astype(BF16), right_rows[k].astype(BF16), ((0,), (0,)))
        if turn + 1 == depth:
            outer_copy = pltpu.make_async_copy(outer, grad_modes_hbm, out_sems.at[1, 0])
            outer_copy.start()
        weights_sum(turn, weight_copies)
        if turn + 1 < depth:
            weight_copies = weights_start(turn + 1)
        finish(coef_copies)

    def place_of(owner):
        place = []
        for at in range(depth - 1, -1, -1):
            place.append((owner // strides[at]) % radices[at])
        return tuple(place)

    for owner in range(size):
        natural[owner * owned:(owner + 1) * owned, :] = gathered[place_of(owner)]

    def spread(step, carry):
        rows = pl.ds(pl.multiple_of(step * chunk, chunk), chunk)
        value = dot(basis[rows, :], natural[...], ((1,), (0,)))
        for s in range(samples):
            result[s, rows, :] = (value[:, s * chan:(s + 1) * chan] + pointwise[s, rows, :]).astype(BF16)
        pltpu.make_async_copy(result.at[:, rows], grad_input_hbm.at[:, rows], out_sems.at[0, step]).start()
        return carry

    for turn in range(depth):
        weight_copies = gather_start(turn, weights_all)
        lax.fori_loop(chunks * turn // depth, chunks * (turn + 1) // depth, spread, 0)
        finish(weight_copies)

    for owner in range(size):
        row = (owner // columns) * rows_each
        target = grad_up if row < chan else grad_down
        row = row % chan
        column = (owner % columns) * wide
        target[row:row + rows_each, column:column + wide] = weights_all[place_of(owner)]

    for step in range(chunks):
        rows = pl.ds(step * chunk, chunk)
        pltpu.make_async_copy(result.at[:, rows], grad_input_hbm.at[:, rows], out_sems.at[0, step]).wait()
    outer_copy.wait()


def per_device(size, inputs, cotangent, basis, mode_weights, w_up, b_up, w_down):
    samples, here, chan = inputs.shape
    hidden_units = w_up.shape[1]
    total_modes = basis.shape[1]
    owned = total_modes // size
    radices = radices_of(size)
    depth = len(radices)
    chunk = min(512, here)
    load_steps = 4
    columns = max(1, 8 * size // (2 * chan))
    rows_each = 2 * chan * columns // size
    wide = hidden_units // columns
    plan = {
        "size": size, "radices": radices, "chunk": chunk,
        "load_steps": load_steps, "columns": columns,
    }
    width = 2 * samples * chan
    shapes, left = [], size
    for radix in reversed(radices):
        left //= radix
        shapes.append((radix, left))
    rows8 = 8 * (-(-3 * samples // 8))
    backwards = tuple(reversed(radices))
    copies = 4 * sum(radix - 1 for radix in radices)
    vmem = pltpu.VMEM
    scratch = [
        vmem((samples, here, chan), BF16),
        vmem((samples, here, chan), BF16),
        vmem((width, here), BF16),
        vmem((here, total_modes), BF16),
        vmem((owned, chan, chan), BF16),
        vmem((width, total_modes), F32),
        vmem((samples, here, chan), F32),
        vmem((samples, here, chan), BF16),
        vmem((owned, chan, chan), F32),
        vmem((chan, hidden_units), F32),
        vmem((chan, hidden_units), F32),
        vmem((8, hidden_units), F32),
        vmem(backwards + (owned, samples * chan), BF16),
        vmem((total_modes, samples * chan), BF16),
        vmem((owned, rows8, chan), F32),
        vmem((owned, rows8, chan), F32),
        vmem((owned, rows8, chan), F32),
        vmem(backwards + (rows_each, wide), F32),
        pltpu.SemaphoreType.DMA((4, load_steps)),
        pltpu.SemaphoreType.DMA((2, here // chunk)),
        pltpu.SemaphoreType.DMA((copies,)),
        pltpu.SemaphoreType.DMA((copies + sum(radix - 1 for radix in radices),)),
    ]
    copies = 5 * sum(radix - 1 for radix in radices)
    scratch[-2] = pltpu.SemaphoreType.DMA((copies,))
    scratch[-1] = pltpu.SemaphoreType.DMA((copies,))
    scratch += [vmem(shape + (owned, width), F32) for shape in shapes]
    scratch += [vmem(shape + (owned, width), BF16) for shape in shapes]
    scratch += [vmem(shape + (owned, width), BF16) for shape in shapes]
    scratch += [vmem(shape + (rows_each, wide), F32) for shape in shapes]
    scratch += [vmem(shape + (rows_each, wide), F32) for shape in shapes]
    scratch += [vmem((shape[0], 8, hidden_units), F32) for shape in shapes]
    anywhere = pl.BlockSpec(memory_space=pl.ANY)
    inside = pl.BlockSpec(memory_space=pltpu.VMEM)
    grad_input, grad_modes, grad_up, grad_bias, grad_down = pl.pallas_call(
        functools.partial(layer_kernel, plan),
        out_shape=(
            jax.ShapeDtypeStruct((samples, here, chan), BF16),
            jax.ShapeDtypeStruct((owned, chan, chan), F32),
            jax.ShapeDtypeStruct((chan, hidden_units), F32),
            jax.ShapeDtypeStruct((1, hidden_units), F32),
            jax.ShapeDtypeStruct((chan, hidden_units), F32),
        ),
        in_specs=[anywhere] * 4 + [inside] * 3,
        out_specs=(anywhere, anywhere, inside, inside, inside),
        scratch_shapes=scratch,
        compiler_params=pltpu.CompilerParams(
            collective_id=0, has_side_effects=True, vmem_limit_bytes=62 * 1024 * 1024
        ),
        name="layer",
    )(inputs, cotangent, basis, mode_weights, w_up, b_up.reshape(1, hidden_units), w_down)
    return grad_input, grad_modes, grad_up, grad_bias.reshape(hidden_units), grad_down.T


def solution(mesh):
    size = mesh.shape["vert"]
    groups = mesh.shape["samp"]

    def body(*arguments):
        grad_input, grad_modes, grad_up, grad_bias, grad_down = per_device(size, *arguments)
        if groups > 1:
            grad_modes, grad_up, grad_bias, grad_down = lax.psum(
                (grad_modes, grad_up, grad_bias, grad_down), "samp"
            )
        return grad_input, grad_modes, grad_up, grad_bias, grad_down

    in_specs = (
        P("samp", "vert", None),
        P("samp", "vert", None),
        P("vert", None),
        P("vert", None, None),
        P(),
        P(),
        P(),
    )
    out_specs = (P("samp", "vert", None), P("vert", None, None), P(), P(), P())
    return jax.shard_map(body, mesh=mesh, in_specs=in_specs, out_specs=out_specs, check_vma=False)
```

```python
import functools

import jax
import jax.numpy as jnp
from jax import lax
from jax.experimental import pallas as pl
from jax.experimental.pallas import tpu as pltpu
from jax.sharding import PartitionSpec as P

F32 = jnp.float32
BF16 = jnp.bfloat16
MESH = pl.DeviceIdType.MESH
ROOT = 0.7978845608
CUBE = 0.044715


def radices_of(size):
    radices = []
    if size % 4 == 0:
        radices.append(4)
        size //= 4
    while size > 1:
        step = 2 if size % 2 == 0 else size
        radices.append(step)
        size //= step
    return tuple(radices) or (1,)


def dot(left, right, contract):
    return lax.dot_general(left, right, (contract, ((), ())), preferred_element_type=F32)


def layer_kernel(
    plan,
    inputs_hbm, cotangent_hbm, basis_hbm, modes_hbm, w_up, b_up, w_down,
    grad_input_hbm, grad_modes_hbm, grad_up, grad_bias, grad_down,
    xs, cs, xt, basis, modes, acc, pointwise, result, outer,
    up_acc, down_acc, bias_acc, gathered, natural, left_rows, right_rows, mixed,
    weights_all, in_sems, out_sems, send_sems, recv_sems, *stages,
):
    size, radices = plan["size"], plan["radices"]
    samples, here, chan = xs.shape
    hidden_units = w_up.shape[1]
    total_modes = basis.shape[1]
    owned = total_modes // size
    depth = len(radices)
    orders = plan["orders"]
    tracks = range(len(orders))
    kinds = [stages[at * depth:(at + 1) * depth] for at in range(len(stages) // depth)]
    coef_f32, coef_send, coef_recv = kinds[0:2], kinds[2:4], kinds[4:6]
    weight_f32, weight_send, weight_recv = kinds[6:8], kinds[8:10], kinds[10:12]
    bias_slots = kinds[12]

    me = lax.axis_index("vert")
    strides = [1] * depth
    for at in range(depth - 2, -1, -1):
        strides[at] = strides[at + 1] * radices[at + 1]
    digits = [lax.rem(lax.div(me, strides[at]), radices[at]) for at in range(depth)]

    def peer(at, shift):
        digit = lax.rem(digits[at] + shift, radices[at])
        return digit, {"vert": me + (digit - digits[at]) * strides[at]}

    load_steps = plan["load_steps"]
    load_rows = here // load_steps

    def loads(step):
        rows = pl.ds(pl.multiple_of(step * load_rows, load_rows), load_rows)
        return (
            pltpu.make_async_copy(inputs_hbm.at[:, rows], xs.at[:, rows], in_sems.at[0, step]),
            pltpu.make_async_copy(cotangent_hbm.at[:, rows], cs.at[:, rows], in_sems.at[1, step]),
            pltpu.make_async_copy(basis_hbm.at[rows], basis.at[rows], in_sems.at[2, step]),
        )

    for step in range(load_steps):
        for copy in loads(step):
            copy.start()
    modes_copy = pltpu.make_async_copy(modes_hbm, modes, in_sems.at[3, 0])
    modes_copy.start()

    barrier = pltpu.get_barrier_semaphore()
    peers = 0
    for at in range(depth):
        for shift in range(1, radices[at]):
            pl.semaphore_signal(barrier, inc=1, device_id=peer(at, shift)[1], device_id_type=MESH)
            peers += 1

    acc[...] = jnp.zeros_like(acc)
    up_acc[...] = jnp.zeros_like(up_acc)
    down_acc[...] = jnp.zeros_like(down_acc)
    bias_acc[...] = jnp.zeros_like(bias_acc)

    def project(step, carry):
        for copy in loads(step):
            copy.wait()
        rows = pl.ds(pl.multiple_of(step * load_rows, load_rows), load_rows)
        for s in range(samples):
            xt[2 * s * chan:(2 * s + 1) * chan, rows] = xs[s, rows, :].T
            xt[(2 * s + 1) * chan:(2 * s + 2) * chan, rows] = cs[s, rows, :].T
        acc[...] += dot(xt[:, rows], basis[rows, :], ((1,), (0,)))
        return carry

    lax.fori_loop(0, load_steps, project, 0)

    def digits_of(owner, order):
        return [(owner // strides[at]) % radices[at] for at in order]

    def slot_of(owner, order):
        found = digits_of(owner, order)
        rest, scale = 0, 1
        for at, digit in zip(order[1:], found[1:]):
            rest += digit * scale
            scale *= radices[at]
        return found[0], rest

    half = acc.shape[0] // len(orders)
    for block in range(total_modes // 128):
        for track in tracks:
            tile = acc[track * half:(track + 1) * half, block * 128:(block + 1) * 128].T
            for part in range(128 // owned):
                owner = block * (128 // owned) + part
                coef_f32[track][0][slot_of(owner, orders[track])] = tile[part * owned:(part + 1) * owned]

    pl.semaphore_wait(barrier, peers)

    sem_at = [0]

    def exchange(at, pairs):
        copies = []
        for shift in range(1, radices[at]):
            digit, target = peer(at, shift)
            for source_of, dest in pairs:
                copies.append(pltpu.make_async_remote_copy(
                    src_ref=source_of(digit),
                    dst_ref=dest,
                    send_sem=send_sems.at[sem_at[0]],
                    recv_sem=recv_sems.at[sem_at[0]],
                    device_id=target,
                    device_id_type=MESH,
                ))
                sem_at[0] += 1
        for copy in copies:
            copy.start()
        return copies

    def finish(copies):
        for copy in copies:
            copy.wait()

    def scatter_start(turn, held, sent, got):
        copies = []
        for track in tracks:
            at = orders[track][turn]
            source = (held if turn == 0 else sent)[track][turn]
            copies += exchange(at, [(lambda digit: source.at[digit], got[track][turn].at[digits[at]])])
        return copies

    def scatter_sum(turn, copies, held, sent, got, done):
        finish(copies)
        for track in tracks:
            order = orders[track]
            at = order[turn]
            for block in range(held[track][turn].shape[1]):
                value = held[track][turn][digits[at], block]
                for shift in range(1, radices[at]):
                    value = value + got[track][turn][peer(at, shift)[0], block].astype(F32)
                if turn + 1 < depth:
                    radix = radices[order[turn + 1]]
                    held[track][turn + 1][block % radix, block // radix] = value
                    sent[track][turn + 1][block % radix, block // radix] = value.astype(BF16)
                else:
                    done(track, value)

    mine = [tuple(digits[at] for at in order) for order in orders]

    def keep_weights(track, value):
        weights_all[(track,) + mine[track]] = value.astype(BF16)

    def weights_start(turn):
        at = orders[0][turn]
        slot = bias_slots[turn].at[digits[at]]
        return scatter_start(turn, weight_f32, weight_send, weight_recv) + exchange(at, [(lambda digit: slot, slot)])

    def weights_sum(turn, copies):
        scatter_sum(turn, copies, weight_f32, weight_send, weight_recv, keep_weights)
        bias = bias_slots[turn][0]
        for slot in range(1, radices[orders[0][turn]]):
            bias = bias + bias_slots[turn][slot]
        if turn + 1 < depth:
            bias_slots[turn + 1][digits[orders[0][turn + 1]]] = bias
        else:
            grad_bias[...] = jnp.sum(bias, axis=0, keepdims=True)

    def gather_start(turn, ref):
        copies = []
        for track in tracks:
            order = orders[track]
            held = ref.at[(track,) + mine[track][:depth - turn]]
            copies += exchange(order[depth - 1 - turn], [(lambda digit: held, held)])
        return copies

    chunk = plan["chunk"]
    chunks = here // chunk

    def point(step, carry):
        rows = pl.ds(pl.multiple_of(step * chunk, chunk), chunk)
        for s in range(samples):
            z = dot(xs[s, rows, :], w_up[...], ((1,), (0,))) + b_up[...]
            square = z * z
            t = jnp.tanh(z * (ROOT + (ROOT * CUBE) * square))
            middle = 0.5 * z
            plus = 1.0 + t
            hidden = (middle * plus).astype(BF16)
            slope = plus * (0.5 + middle * (1.0 - t) * (ROOT + (3.0 * ROOT * CUBE) * square))
            grad_hidden = dot(cs[s, rows, :], w_down[...], ((1,), (1,)))
            grad_pre = (grad_hidden * slope).astype(BF16)
            pointwise[s, rows, :] = dot(grad_pre, w_up[...], ((1,), (1,)))
            up_acc[...] += dot(xt[2 * s * chan:(2 * s + 1) * chan, rows], grad_pre, ((1,), (0,)))
            down_acc[...] += dot(xt[(2 * s + 1) * chan:(2 * s + 2) * chan, rows], hidden, ((1,), (0,)))
            bias_acc[...] += jnp.sum(grad_pre.astype(F32).reshape(chunk // 8, 8, hidden_units), axis=0)
        return carry

    totals = []
    for turn in range(depth):
        copies = scatter_start(turn, coef_f32, coef_send, coef_recv)
        lax.fori_loop(chunks * turn // depth, chunks * (turn + 1) // depth, point, 0)
        scatter_sum(turn, copies, coef_f32, coef_send, coef_recv, lambda track, value: totals.append(value))
    owned_sums = jnp.concatenate(totals, axis=1)

    columns = plan["columns"]
    rows_each = 2 * chan * columns // size
    wide = hidden_units // columns
    part_wide = wide // len(orders)
    for owner in range(size):
        row = (owner // columns) * rows_each
        source = up_acc if row < chan else down_acc
        row = row % chan
        column = (owner % columns) * wide
        for track in tracks:
            start = column + track * part_wide
            weight_f32[track][0][slot_of(owner, orders[track])] = source[row:row + rows_each, start:start + part_wide]
    bias_slots[0][digits[orders[0][0]]] = bias_acc[...]

    weight_copies = weights_start(0)

    left_rows[...] = jnp.zeros_like(left_rows)
    right_rows[...] = jnp.zeros_like(right_rows)
    for s in range(samples):
        coef = owned_sums[:, 2 * s * chan:(2 * s + 1) * chan]
        grad = owned_sums[:, (2 * s + 1) * chan:(2 * s + 2) * chan]
        coef_high = coef.astype(BF16).astype(F32)
        grad_high = grad.astype(BF16).astype(F32)
        left_rows[:, s, :] = coef_high
        left_rows[:, samples + s, :] = coef_high
        left_rows[:, 2 * samples + s, :] = coef - coef_high
        right_rows[:, s, :] = grad_high
        right_rows[:, samples + s, :] = grad - grad_high
        right_rows[:, 2 * samples + s, :] = grad_high
    modes_copy.wait()
    for k in range(owned):
        mixed[k] = dot(right_rows[k].astype(BF16), modes[k], ((1,), (1,)))
    value = jnp.concatenate([mixed[:, s, :] + mixed[:, samples + s, :] for s in range(samples)], axis=1)
    part_chan = samples * chan // len(orders)
    for track in tracks:
        gathered[(track,) + mine[track]] = value[:, track * part_chan:(track + 1) * part_chan].astype(BF16)

    per_turn = -(-owned // depth)
    for turn in range(depth):
        coef_copies = gather_start(turn, gathered)
        for k in range(turn * per_turn, min(owned, (turn + 1) * per_turn)):
            outer[k] = dot(left_rows[k].astype(BF16), right_rows[k].astype(BF16), ((0,), (0,)))
        if turn + 1 == depth:
            outer_copy = pltpu.make_async_copy(outer, grad_modes_hbm, out_sems.at[1, 0])
            outer_copy.start()
        weights_sum(turn, weight_copies)
        if turn + 1 < depth:
            weight_copies = weights_start(turn + 1)
        finish(coef_copies)

    for owner in range(size):
        for track in tracks:
            natural[owner * owned:(owner + 1) * owned, track * part_chan:(track + 1) * part_chan] = gathered[
                (track,) + tuple(digits_of(owner, orders[track]))]

    def spread(step, carry):
        rows = pl.ds(pl.multiple_of(step * chunk, chunk), chunk)
        value = dot(basis[rows, :], natural[...], ((1,), (0,)))
        for s in range(samples):
            result[s, rows, :] = (value[:, s * chan:(s + 1) * chan] + pointwise[s, rows, :]).astype(BF16)
        pltpu.make_async_copy(result.at[:, rows], grad_input_hbm.at[:, rows], out_sems.at[0, step]).start()
        return carry

    for turn in range(depth):
        weight_copies = gather_start(turn, weights_all)
        lax.fori_loop(chunks * turn // depth, chunks * (turn + 1) // depth, spread, 0)
        finish(weight_copies)

    for owner in range(size):
        row = (owner // columns) * rows_each
        target = grad_up if row < chan else grad_down
        row = row % chan
        column = (owner % columns) * wide
        for track in tracks:
            start = column + track * part_wide
            target[row:row + rows_each, start:start + part_wide] = weights_all[
                (track,) + tuple(digits_of(owner, orders[track]))].astype(F32)

    for step in range(chunks):
        rows = pl.ds(step * chunk, chunk)
        pltpu.make_async_copy(result.at[:, rows], grad_input_hbm.at[:, rows], out_sems.at[0, step]).wait()
    outer_copy.wait()


def place_kernel(
    steps, input_from, modes_from, up_from, bias_from, down_from,
    input_to, modes_to, up_to, bias_to, down_to, input_held, modes_held, sems,
):
    def parts(step):
        rows = input_held.shape[1] // steps
        here = pl.ds(step * rows, rows)
        kept = modes_held.shape[0] // steps
        modes = pl.ds(step * kept, kept)
        return (
            (input_from.at[:, here], input_held.at[:, here], input_to.at[:, here]),
            (modes_from.at[modes], modes_held.at[modes], modes_to.at[modes]),
        )

    reads, writes = [], []
    for step in range(steps):
        for kind, (source, held, target) in enumerate(parts(step)):
            reads.append(pltpu.make_async_copy(source, held, sems.at[kind, step]))
            writes.append(pltpu.make_async_copy(held, target, sems.at[2 + kind, step]))
    for copy in reads:
        copy.start()
    up_to[...] = up_from[...]
    bias_to[...] = bias_from[...]
    down_to[...] = down_from[...].T
    for read, write in zip(reads, writes):
        read.wait()
        write.start()
    for write in writes:
        write.wait()


def per_device(size, inputs, cotangent, basis, mode_weights, w_up, b_up, w_down):
    samples, here, chan = inputs.shape
    hidden_units = w_up.shape[1]
    total_modes = basis.shape[1]
    owned = total_modes // size
    radices = radices_of(size)
    depth = len(radices)
    chunk = min(512, here)
    load_steps = 4
    columns = max(1, min(16 * size // (2 * chan), hidden_units // 256))
    rows_each = 2 * chan * columns // size
    wide = hidden_units // columns
    plan = {
        "size": size, "radices": radices, "chunk": chunk,
        "load_steps": load_steps, "columns": columns,
    }
    width = 2 * samples * chan
    straight = list(reversed(range(depth)))
    crossed = list(straight)
    if depth > 2:
        crossed[1], crossed[2] = crossed[2], crossed[1]
    orders = (tuple(straight), tuple(crossed))
    plan["orders"] = orders
    shapes = []
    for order in orders:
        left, found = size, []
        for at in order:
            left //= radices[at]
            found.append((radices[at], left))
        shapes.append(found)
    rows8 = 8 * (-(-3 * samples // 8))
    backwards = tuple(radices[at] for at in orders[0])
    other = tuple(radices[at] for at in orders[1])
    assert backwards == other
    copies = 9 * sum(radix - 1 for radix in radices)
    vmem = pltpu.VMEM
    scratch = [
        vmem((samples, here, chan), BF16),
        vmem((samples, here, chan), BF16),
        vmem((width, here), BF16),
        vmem((here, total_modes), BF16),
        vmem((owned, chan, chan), BF16),
        vmem((width, total_modes), F32),
        vmem((samples, here, chan), F32),
        vmem((samples, here, chan), BF16),
        vmem((owned, chan, chan), F32),
        vmem((chan, hidden_units), F32),
        vmem((chan, hidden_units), F32),
        vmem((8, hidden_units), F32),
        vmem((2,) + backwards + (owned, samples * chan // 2), BF16),
        vmem((total_modes, samples * chan), BF16),
        vmem((owned, rows8, chan), F32),
        vmem((owned, rows8, chan), F32),
        vmem((owned, rows8, chan), F32),
        vmem((2,) + backwards + (rows_each, wide // 2), BF16),
        pltpu.SemaphoreType.DMA((4, load_steps)),
        pltpu.SemaphoreType.DMA((2, here // chunk)),
        pltpu.SemaphoreType.DMA((copies,)),
        pltpu.SemaphoreType.DMA((copies,)),
    ]

    def stage_buffers(tail, first_type, later_type):
        return [
            vmem(shape + tail, later_type if turn else first_type)
            for found in shapes for turn, shape in enumerate(found)
        ]

    for tail in ((owned, width // 2), (rows_each, wide // 2)):
        scratch += stage_buffers(tail, F32, F32)
        scratch += stage_buffers(tail, BF16, BF16)
        scratch += stage_buffers(tail, F32, BF16)
    scratch += [vmem((shape[0], 8, hidden_units), F32) for shape in shapes[0]]
    anywhere = pl.BlockSpec(memory_space=pl.ANY)
    inside = pl.BlockSpec(memory_space=pltpu.VMEM)
    grad_input, grad_modes, grad_up, grad_bias, grad_down = pl.pallas_call(
        functools.partial(layer_kernel, plan),
        out_shape=(
            jax.ShapeDtypeStruct((samples, here, chan), BF16),
            jax.ShapeDtypeStruct((owned, chan, chan), F32),
            jax.ShapeDtypeStruct((chan, hidden_units), F32),
            jax.ShapeDtypeStruct((1, hidden_units), F32),
            jax.ShapeDtypeStruct((chan, hidden_units), F32),
        ),
        in_specs=[anywhere] * 4 + [inside] * 3,
        out_specs=(anywhere, anywhere, inside, inside, inside),
        scratch_shapes=scratch,
        compiler_params=pltpu.CompilerParams(
            collective_id=0, has_side_effects=True, vmem_limit_bytes=62 * 1024 * 1024
        ),
        name="layer",
    )(inputs, cotangent, basis, mode_weights, w_up, b_up.reshape(1, hidden_units), w_down)
    steps = 4
    grad_input, grad_modes, grad_up, grad_bias, grad_down = pl.pallas_call(
        functools.partial(place_kernel, steps),
        out_shape=(
            jax.ShapeDtypeStruct((samples, here, chan), BF16),
            jax.ShapeDtypeStruct((owned, chan, chan), F32),
            jax.ShapeDtypeStruct((chan, hidden_units), F32),
            jax.ShapeDtypeStruct((1, hidden_units), F32),
            jax.ShapeDtypeStruct((hidden_units, chan), F32),
        ),
        in_specs=[anywhere] * 2 + [inside] * 3,
        out_specs=(anywhere, anywhere, inside, inside, inside),
        scratch_shapes=[
            vmem((samples, here, chan), BF16),
            vmem((owned, chan, chan), F32),
            pltpu.SemaphoreType.DMA((4, steps)),
        ],
        compiler_params=pltpu.CompilerParams(vmem_limit_bytes=16 * 1024 * 1024),
        name="place",
    )(grad_input, grad_modes, grad_up, grad_bias, grad_down)
    return grad_input, grad_modes, grad_up, grad_bias.reshape(hidden_units), grad_down


def solution(mesh):
    size = mesh.shape["vert"]
    groups = mesh.shape["samp"]

    def body(*arguments):
        grad_input, grad_modes, grad_up, grad_bias, grad_down = per_device(size, *arguments)
        if groups > 1:
            grad_modes, grad_up, grad_bias, grad_down = lax.psum(
                (grad_modes, grad_up, grad_bias, grad_down), "samp"
            )
        return grad_input, grad_modes, grad_up, grad_bias, grad_down

    in_specs = (
        P("samp", "vert", None),
        P("samp", "vert", None),
        P("vert", None),
        P("vert", None, None),
        P(),
        P(),
        P(),
    )
    out_specs = (P("samp", "vert", None), P("vert", None, None), P(), P(), P())
    return jax.shard_map(body, mesh=mesh, in_specs=in_specs, out_specs=out_specs, check_vma=False)
```

```python
import functools

import jax
import jax.numpy as jnp
from jax import lax
from jax.experimental import pallas as pl
from jax.experimental.pallas import tpu as pltpu
from jax.sharding import PartitionSpec as P

F32 = jnp.float32
BF16 = jnp.bfloat16
MESH = pl.DeviceIdType.MESH
ROOT = 0.7978845608
CUBE = 0.044715


def radices_of(size):
    radices = []
    if size % 4 == 0:
        radices.append(4)
        size //= 4
    while size > 1:
        step = 2 if size % 2 == 0 else size
        radices.append(step)
        size //= step
    return tuple(radices) or (1,)


def dot(left, right, contract):
    return lax.dot_general(left, right, (contract, ((), ())), preferred_element_type=F32)


def layer_kernel(
    plan,
    inputs_hbm, cotangent_hbm, basis_hbm, modes_hbm, w_up, b_up, w_down,
    grad_input_hbm, grad_modes_hbm, grad_up, grad_bias, grad_down,
    xs, cs, xt, basis, modes, acc, pointwise, result, outer,
    up_acc, down_acc, bias_acc, gathered, natural, left_rows, right_rows, mixed,
    weights_all, in_sems, out_sems, send_sems, recv_sems, *stages,
):
    size, radices = plan["size"], plan["radices"]
    samples, here, chan = xs.shape
    hidden_units = w_up.shape[1]
    total_modes = basis.shape[1]
    owned = total_modes // size
    depth = len(radices)
    orders = plan["orders"]
    tracks = range(len(orders))
    kinds = [stages[at * depth:(at + 1) * depth] for at in range(len(stages) // depth)]
    coef_f32, coef_send, coef_recv = kinds[0:2], kinds[2:4], kinds[4:6]
    weight_f32, weight_send, weight_recv = kinds[6:8], kinds[8:10], kinds[10:12]
    bias_slots = kinds[12]

    me = lax.axis_index("vert")
    strides = [1] * depth
    for at in range(depth - 2, -1, -1):
        strides[at] = strides[at + 1] * radices[at + 1]
    digits = [lax.rem(lax.div(me, strides[at]), radices[at]) for at in range(depth)]

    def peer(at, shift):
        digit = lax.rem(digits[at] + shift, radices[at])
        return digit, {"vert": me + (digit - digits[at]) * strides[at]}

    load_steps = plan["load_steps"]
    load_rows = here // load_steps

    def loads(step):
        rows = pl.ds(pl.multiple_of(step * load_rows, load_rows), load_rows)
        return (
            pltpu.make_async_copy(inputs_hbm.at[:, rows], xs.at[:, rows], in_sems.at[0, step]),
            pltpu.make_async_copy(cotangent_hbm.at[:, rows], cs.at[:, rows], in_sems.at[1, step]),
            pltpu.make_async_copy(basis_hbm.at[rows], basis.at[rows], in_sems.at[2, step]),
        )

    for step in range(load_steps):
        for copy in loads(step):
            copy.start()
    modes_copy = pltpu.make_async_copy(modes_hbm, modes, in_sems.at[3, 0])
    modes_copy.start()

    barrier = pltpu.get_barrier_semaphore()
    peers = 0
    for at in range(depth):
        for shift in range(1, radices[at]):
            pl.semaphore_signal(barrier, inc=1, device_id=peer(at, shift)[1], device_id_type=MESH)
            peers += 1

    acc[...] = jnp.zeros_like(acc)
    up_acc[...] = jnp.zeros_like(up_acc)
    down_acc[...] = jnp.zeros_like(down_acc)
    bias_acc[...] = jnp.zeros_like(bias_acc)

    def project(step, carry):
        for copy in loads(step):
            copy.wait()
        rows = pl.ds(pl.multiple_of(step * load_rows, load_rows), load_rows)
        for s in range(samples):
            xt[2 * s * chan:(2 * s + 1) * chan, rows] = xs[s, rows, :].T
            xt[(2 * s + 1) * chan:(2 * s + 2) * chan, rows] = cs[s, rows, :].T
        acc[...] += dot(xt[:, rows], basis[rows, :], ((1,), (0,)))
        return carry

    lax.fori_loop(0, load_steps, project, 0)

    def digits_of(owner, order):
        return [(owner // strides[at]) % radices[at] for at in order]

    def slot_of(owner, order):
        found = digits_of(owner, order)
        rest, scale = 0, 1
        for at, digit in zip(order[1:], found[1:]):
            rest += digit * scale
            scale *= radices[at]
        return found[0], rest

    half = acc.shape[0] // len(orders)
    for block in range(total_modes // 128):
        for track in tracks:
            tile = acc[track * half:(track + 1) * half, block * 128:(block + 1) * 128].T
            for part in range(128 // owned):
                owner = block * (128 // owned) + part
                coef_f32[track][0][slot_of(owner, orders[track])] = tile[part * owned:(part + 1) * owned]

    pl.semaphore_wait(barrier, peers)

    sem_at = [0]

    def exchange(at, pairs):
        copies = []
        for shift in range(1, radices[at]):
            digit, target = peer(at, shift)
            for source_of, dest in pairs:
                copies.append(pltpu.make_async_remote_copy(
                    src_ref=source_of(digit),
                    dst_ref=dest,
                    send_sem=send_sems.at[sem_at[0]],
                    recv_sem=recv_sems.at[sem_at[0]],
                    device_id=target,
                    device_id_type=MESH,
                ))
                sem_at[0] += 1
        for copy in copies:
            copy.start()
        return copies

    def finish(copies):
        for copy in copies:
            copy.wait()

    def scatter_start(turn, held, sent, got):
        copies = []
        for track in tracks:
            at = orders[track][turn]
            source = (held if turn == 0 else sent)[track][turn]
            copies += exchange(at, [(lambda digit: source.at[digit], got[track][turn].at[digits[at]])])
        return copies

    def scatter_sum(turn, copies, held, sent, got, done):
        finish(copies)
        for track in tracks:
            order = orders[track]
            at = order[turn]
            for block in range(held[track][turn].shape[1]):
                value = held[track][turn][digits[at], block]
                for shift in range(1, radices[at]):
                    value = value + got[track][turn][peer(at, shift)[0], block].astype(F32)
                if turn + 1 < depth:
                    radix = radices[order[turn + 1]]
                    held[track][turn + 1][block % radix, block // radix] = value
                    sent[track][turn + 1][block % radix, block // radix] = value.astype(BF16)
                else:
                    done(track, value)

    mine = [tuple(digits[at] for at in order) for order in orders]

    def keep_weights(track, value):
        weights_all[(track,) + mine[track]] = value.astype(BF16)

    def weights_start(turn):
        at = orders[0][turn]
        slot = bias_slots[turn].at[digits[at]]
        return scatter_start(turn, weight_f32, weight_send, weight_recv) + exchange(at, [(lambda digit: slot, slot)])

    def weights_sum(turn, copies):
        scatter_sum(turn, copies, weight_f32, weight_send, weight_recv, keep_weights)
        bias = bias_slots[turn][0]
        for slot in range(1, radices[orders[0][turn]]):
            bias = bias + bias_slots[turn][slot]
        if turn + 1 < depth:
            bias_slots[turn + 1][digits[orders[0][turn + 1]]] = bias
        else:
            grad_bias[...] = jnp.sum(bias, axis=0, keepdims=True)

    def gather_start(turn, ref):
        copies = []
        for track in tracks:
            order = orders[track]
            held = ref.at[(track,) + mine[track][:depth - turn]]
            copies += exchange(order[depth - 1 - turn], [(lambda digit: held, held)])
        return copies

    chunk = plan["chunk"]
    chunks = here // chunk

    def point(step, carry):
        rows = pl.ds(pl.multiple_of(step * chunk, chunk), chunk)
        for s in range(samples):
            z = dot(xs[s, rows, :], w_up[...], ((1,), (0,))) + b_up[...]
            square = z * z
            t = jnp.tanh(z * (ROOT + (ROOT * CUBE) * square))
            middle = 0.5 * z
            plus = 1.0 + t
            hidden = (middle * plus).astype(BF16)
            slope = plus * (0.5 + middle * (1.0 - t) * (ROOT + (3.0 * ROOT * CUBE) * square))
            grad_hidden = dot(cs[s, rows, :], w_down[...], ((1,), (1,)))
            grad_pre = (grad_hidden * slope).astype(BF16)
            pointwise[s, rows, :] = dot(grad_pre, w_up[...], ((1,), (1,)))
            up_acc[...] += dot(xt[2 * s * chan:(2 * s + 1) * chan, rows], grad_pre, ((1,), (0,)))
            down_acc[...] += dot(xt[(2 * s + 1) * chan:(2 * s + 2) * chan, rows], hidden, ((1,), (0,)))
            bias_acc[...] += jnp.sum(grad_pre.astype(F32).reshape(chunk // 8, 8, hidden_units), axis=0)
        return carry

    totals = []
    for turn in range(depth):
        copies = scatter_start(turn, coef_f32, coef_send, coef_recv)
        lax.fori_loop(chunks * turn // depth, chunks * (turn + 1) // depth, point, 0)
        scatter_sum(turn, copies, coef_f32, coef_send, coef_recv, lambda track, value: totals.append(value))
    owned_sums = jnp.concatenate(totals, axis=1)

    columns = plan["columns"]
    rows_each = 2 * chan * columns // size
    wide = hidden_units // columns
    part_wide = wide // len(orders)
    for owner in range(size):
        row = (owner // columns) * rows_each
        source = up_acc if row < chan else down_acc
        row = row % chan
        column = (owner % columns) * wide
        for track in tracks:
            start = column + track * part_wide
            weight_f32[track][0][slot_of(owner, orders[track])] = source[row:row + rows_each, start:start + part_wide]
    bias_slots[0][digits[orders[0][0]]] = bias_acc[...]

    weight_copies = weights_start(0)

    left_rows[...] = jnp.zeros_like(left_rows)
    right_rows[...] = jnp.zeros_like(right_rows)
    for s in range(samples):
        coef = owned_sums[:, 2 * s * chan:(2 * s + 1) * chan]
        grad = owned_sums[:, (2 * s + 1) * chan:(2 * s + 2) * chan]
        coef_high = coef.astype(BF16).astype(F32)
        grad_high = grad.astype(BF16).astype(F32)
        left_rows[:, s, :] = coef_high
        left_rows[:, samples + s, :] = coef_high
        left_rows[:, 2 * samples + s, :] = coef - coef_high
        right_rows[:, s, :] = grad_high
        right_rows[:, samples + s, :] = grad - grad_high
        right_rows[:, 2 * samples + s, :] = grad_high
    modes_copy.wait()
    for k in range(owned):
        mixed[k] = dot(right_rows[k].astype(BF16), modes[k], ((1,), (1,)))
    value = jnp.concatenate([mixed[:, s, :] + mixed[:, samples + s, :] for s in range(samples)], axis=1)
    part_chan = samples * chan // len(orders)
    for track in tracks:
        gathered[(track,) + mine[track]] = value[:, track * part_chan:(track + 1) * part_chan].astype(BF16)

    per_turn = -(-owned // depth)
    for turn in range(depth):
        coef_copies = gather_start(turn, gathered)
        for k in range(turn * per_turn, min(owned, (turn + 1) * per_turn)):
            outer[k] = dot(left_rows[k].astype(BF16), right_rows[k].astype(BF16), ((0,), (0,)))
        if turn + 1 == depth:
            outer_copy = pltpu.make_async_copy(outer, grad_modes_hbm, out_sems.at[1, 0])
            outer_copy.start()
        weights_sum(turn, weight_copies)
        if turn + 1 < depth:
            weight_copies = weights_start(turn + 1)
        finish(coef_copies)

    for owner in range(size):
        for track in tracks:
            natural[owner * owned:(owner + 1) * owned, track * part_chan:(track + 1) * part_chan] = gathered[
                (track,) + tuple(digits_of(owner, orders[track]))]

    def spread(step, carry):
        rows = pl.ds(pl.multiple_of(step * chunk, chunk), chunk)
        value = dot(basis[rows, :], natural[...], ((1,), (0,)))
        for s in range(samples):
            result[s, rows, :] = (value[:, s * chan:(s + 1) * chan] + pointwise[s, rows, :]).astype(BF16)
        pltpu.make_async_copy(result.at[:, rows], grad_input_hbm.at[:, rows], out_sems.at[0, step]).start()
        return carry

    for turn in range(depth):
        weight_copies = gather_start(turn, weights_all)
        lax.fori_loop(chunks * turn // depth, chunks * (turn + 1) // depth, spread, 0)
        finish(weight_copies)

    for owner in range(size):
        row = (owner // columns) * rows_each
        target = grad_up if row < chan else grad_down
        row = row % chan
        column = (owner % columns) * wide
        for track in tracks:
            start = column + track * part_wide
            target[row:row + rows_each, start:start + part_wide] = weights_all[
                (track,) + tuple(digits_of(owner, orders[track]))].astype(F32)

    for step in range(chunks):
        rows = pl.ds(step * chunk, chunk)
        pltpu.make_async_copy(result.at[:, rows], grad_input_hbm.at[:, rows], out_sems.at[0, step]).wait()
    outer_copy.wait()


def place_kernel(
    steps, input_from, modes_from, up_from, bias_from, down_from,
    input_to, modes_to, up_to, bias_to, down_to, input_held, modes_held, sems,
):
    def parts(step):
        rows = input_held.shape[1] // steps
        here = pl.ds(step * rows, rows)
        kept = modes_held.shape[0] // steps
        modes = pl.ds(step * kept, kept)
        return (
            (input_from.at[:, here], input_held.at[:, here], input_to.at[:, here]),
            (modes_from.at[modes], modes_held.at[modes], modes_to.at[modes]),
        )

    reads, writes = [], []
    for step in range(steps):
        for kind, (source, held, target) in enumerate(parts(step)):
            reads.append(pltpu.make_async_copy(source, held, sems.at[kind, step]))
            writes.append(pltpu.make_async_copy(held, target, sems.at[2 + kind, step]))
    for copy in reads:
        copy.start()
    up_to[...] = up_from[...]
    bias_to[...] = bias_from[...]
    down_to[...] = down_from[...].T
    for read, write in zip(reads, writes):
        read.wait()
        write.start()
    for write in writes:
        write.wait()


def per_device(size, inputs, cotangent, basis, mode_weights, w_up, b_up, w_down):
    samples, here, chan = inputs.shape
    hidden_units = w_up.shape[1]
    total_modes = basis.shape[1]
    owned = total_modes // size
    radices = radices_of(size)
    depth = len(radices)
    chunk = min(512, here)
    load_steps = 4
    columns = max(1, min(16 * size // (2 * chan), hidden_units // 256))
    rows_each = 2 * chan * columns // size
    wide = hidden_units // columns
    plan = {
        "size": size, "radices": radices, "chunk": chunk,
        "load_steps": load_steps, "columns": columns,
    }
    width = 2 * samples * chan
    straight = list(reversed(range(depth)))
    crossed = list(straight)
    if depth > 2:
        crossed[1], crossed[2] = crossed[2], crossed[1]
    orders = (tuple(straight), tuple(crossed))
    plan["orders"] = orders
    shapes = []
    for order in orders:
        left, found = size, []
        for at in order:
            left //= radices[at]
            found.append((radices[at], left))
        shapes.append(found)
    rows8 = 8 * (-(-3 * samples // 8))
    backwards = tuple(radices[at] for at in orders[0])
    other = tuple(radices[at] for at in orders[1])
    assert backwards == other
    copies = 9 * sum(radix - 1 for radix in radices)
    vmem = pltpu.VMEM
    scratch = [
        vmem((samples, here, chan), BF16),
        vmem((samples, here, chan), BF16),
        vmem((width, here), BF16),
        vmem((here, total_modes), BF16),
        vmem((owned, chan, chan), BF16),
        vmem((width, total_modes), F32),
        vmem((samples, here, chan), F32),
        vmem((samples, here, chan), BF16),
        vmem((owned, chan, chan), F32),
        vmem((chan, hidden_units), F32),
        vmem((chan, hidden_units), F32),
        vmem((8, hidden_units), F32),
        vmem((2,) + backwards + (owned, samples * chan // 2), BF16),
        vmem((total_modes, samples * chan), BF16),
        vmem((owned, rows8, chan), F32),
        vmem((owned, rows8, chan), F32),
        vmem((owned, rows8, chan), F32),
        vmem((2,) + backwards + (rows_each, wide // 2), BF16),
        pltpu.SemaphoreType.DMA((4, load_steps)),
        pltpu.SemaphoreType.DMA((2, here // chunk)),
        pltpu.SemaphoreType.DMA((copies,)),
        pltpu.SemaphoreType.DMA((copies,)),
    ]

    def stage_buffers(tail, first_type, later_type):
        return [
            vmem(shape + tail, later_type if turn else first_type)
            for found in shapes for turn, shape in enumerate(found)
        ]

    for tail in ((owned, width // 2), (rows_each, wide // 2)):
        scratch += stage_buffers(tail, F32, F32)
        scratch += stage_buffers(tail, BF16, BF16)
        scratch += stage_buffers(tail, F32, BF16)
    scratch += [vmem((shape[0], 8, hidden_units), F32) for shape in shapes[0]]
    anywhere = pl.BlockSpec(memory_space=pl.ANY)
    inside = pl.BlockSpec(memory_space=pltpu.VMEM)
    grad_input, grad_modes, grad_up, grad_bias, grad_down = pl.pallas_call(
        functools.partial(layer_kernel, plan),
        out_shape=(
            jax.ShapeDtypeStruct((samples, here, chan), BF16),
            jax.ShapeDtypeStruct((owned, chan, chan), F32),
            jax.ShapeDtypeStruct((chan, hidden_units), F32),
            jax.ShapeDtypeStruct((1, hidden_units), F32),
            jax.ShapeDtypeStruct((chan, hidden_units), F32),
        ),
        in_specs=[anywhere] * 4 + [inside] * 3,
        out_specs=(anywhere, anywhere, inside, inside, inside),
        scratch_shapes=scratch,
        compiler_params=pltpu.CompilerParams(
            collective_id=0, has_side_effects=True, vmem_limit_bytes=62 * 1024 * 1024
        ),
        name="layer",
    )(inputs, cotangent, basis, mode_weights, w_up, b_up.reshape(1, hidden_units), w_down)
    steps = 4
    grad_input, grad_modes, grad_up, grad_bias, grad_down = pl.pallas_call(
        functools.partial(place_kernel, steps),
        out_shape=(
            jax.ShapeDtypeStruct((samples, here, chan), BF16),
            jax.ShapeDtypeStruct((owned, chan, chan), F32),
            jax.ShapeDtypeStruct((chan, hidden_units), F32),
            jax.ShapeDtypeStruct((1, hidden_units), F32),
            jax.ShapeDtypeStruct((hidden_units, chan), F32),
        ),
        in_specs=[anywhere] * 2 + [inside] * 3,
        out_specs=(anywhere, anywhere, inside, inside, inside),
        scratch_shapes=[
            vmem((samples, here, chan), BF16),
            vmem((owned, chan, chan), F32),
            pltpu.SemaphoreType.DMA((4, steps)),
        ],
        compiler_params=pltpu.CompilerParams(vmem_limit_bytes=62 * 1024 * 1024),
        name="place",
    )(grad_input, grad_modes, grad_up, grad_bias, grad_down)
    return grad_input, grad_modes, grad_up, grad_bias.reshape(hidden_units), grad_down


def solution(mesh):
    size = mesh.shape["vert"]
    groups = mesh.shape["samp"]

    def body(*arguments):
        grad_input, grad_modes, grad_up, grad_bias, grad_down = per_device(size, *arguments)
        if groups > 1:
            grad_modes, grad_up, grad_bias, grad_down = lax.psum(
                (grad_modes, grad_up, grad_bias, grad_down), "samp"
            )
        return grad_input, grad_modes, grad_up, grad_bias, grad_down

    in_specs = (
        P("samp", "vert", None),
        P("samp", "vert", None),
        P("vert", None),
        P("vert", None, None),
        P(),
        P(),
        P(),
    )
    out_specs = (P("samp", "vert", None), P("vert", None, None), P(), P(), P())
    return jax.shard_map(body, mesh=mesh, in_specs=in_specs, out_specs=out_specs, check_vma=False)
```
